256 devices in a mesh: seq: 128 (over y, z, x), head: 2 (over core).
Axes of the slice: x: 4, y: 4, z: 8, core: 2. Of those that a mesh axis runs over, the one named last changes fastest.
Arguments:
- queries: bfloat16 [16384, 2048], P('seq', 'head'), may hold values from -8 to 8
- key_tokens: bfloat16 [16384, 2048], P('seq', 'head'), may hold values from -8 to 8
- value_tokens: bfloat16 [16384, 2048], P('seq', 'head'), may hold values from -6 to 6
- out_weight: bfloat16 [2048, 2048], P(None, 'head'), may hold values from -0.125 to 0.125
- output_grad: bfloat16 [16384, 2048], P('seq', 'head'), may hold values from -6 to 6
Outputs:
- output: bfloat16 [16384, 2048], P('seq', 'head')
- query_grad: bfloat16 [16384, 2048], P('seq', 'head')
- key_grad: bfloat16 [16384, 2048], P('seq', 'head')
- value_grad: bfloat16 [16384, 2048], P('seq', 'head')
The draws below stay inside these ranges and needn't reach their ends.
All inputs are finite; a program needn't handle non-finite values.
Results may differ from the reference program's by a relative error of at most 0.024.
Values may be sent and summed in bfloat16 or wider, within the bound.
A program may use at most 128 MiB of HBM per device.

```python
import jax
import jax.numpy as jnp
from jax import lax

D = 2048
HEADS = 16
HDIM = 128
BLOCK = 128
TOK_DEV = 128
SLABS = 128
LEVELS = 7
TOKENS = 16384


def base_field(key):
    return jnp.clip(jax.random.normal(key, (TOKENS, D), jnp.float32), -6.0, 6.0)


def draw_queries(key, part):
    field = base_field(jax.random.fold_in(key, 11))
    return field.astype(jnp.bfloat16)


def draw_key_tokens(key, part):
    field = base_field(jax.random.fold_in(key, 23))
    return field.astype(jnp.bfloat16)


def block_scale(own_key, shape, pieces, smallest, high):
    def one(dim, blocks):
        draws = jax.random.uniform(jax.random.fold_in(jax.random.fold_in(own_key, 6), dim), (blocks,), jnp.float32, smallest / len(pieces), high / len(pieces))
        return jnp.repeat(jnp.exp(draws), shape[dim] // blocks).reshape((-1,) + (1,) * (len(shape) - dim - 1))

    loudness = one(*pieces[0])
    for cut in pieces[1:]:
        loudness = loudness * one(*cut)
    return loudness


def scatter_about(own_key, extent, deviation, bound, shards=(), kind=jnp.bfloat16):
    entries = deviation * jax.random.normal(own_key, extent, jnp.float32)
    if shards:
        entries = entries * block_scale(own_key, extent, shards, -0.22, 0.18)
    return jnp.clip(entries, -bound, bound).astype(kind)


def setup_inputs(seed: int = 0) -> dict:
    keys = jax.random.split(jax.random.key(seed), 6)
    queries = draw_queries(jax.random.fold_in(keys[5], 71), 0)
    key_tokens = draw_key_tokens(jax.random.fold_in(keys[5], 71), 0)
    value_tokens = scatter_about(keys[2], (TOKENS, D), 1.0, 6.0, ((0, 128), (1, 2)))
    out_weight = scatter_about(keys[3], (D, D), D ** -0.5, 0.125, ((1, 2),))
    output_grad = scatter_about(keys[4], (TOKENS, D), 1.0, 6.0, ((0, 128), (1, 2)))
    return {"queries": queries, "key_tokens": key_tokens, "value_tokens": value_tokens, "out_weight": out_weight, "output_grad": output_grad}


def coarsen(tokens, run_length, summed):
    grouped = tokens.astype(jnp.float32).reshape(-1, run_length, tokens.shape[1])
    if summed:
        reduced = jnp.sum(grouped, axis=1)
    else:
        reduced = jnp.mean(grouped, axis=1)
    return reduced.astype(jnp.bfloat16)


def reference(queries, key_tokens, value_tokens, out_weight, output_grad):
    run_lengths = [(TOK_DEV << level) // BLOCK for level in range(LEVELS)]
    coarse_keys = [coarsen(key_tokens, run_lengths[level], False) for level in range(LEVELS)]
    coarse_values = [coarsen(value_tokens, run_lengths[level], True) for level in range(LEVELS)]
    grad_attended = jnp.dot(output_grad, out_weight, preferred_element_type=jnp.float32).astype(jnp.bfloat16)
    inv_scale = 1.0 / float(HDIM) ** 0.5
    list_rows = TOK_DEV + LEVELS * BLOCK

    def slab_step(carry, slab):
        key_accum, value_accum = carry
        start = (slab * TOK_DEV).astype(jnp.int32)
        query_slab = lax.dynamic_slice_in_dim(queries, start, TOK_DEV, 0)
        key_parts = [lax.dynamic_slice_in_dim(key_tokens, start, TOK_DEV, 0)]
        value_parts = [lax.dynamic_slice_in_dim(value_tokens, start, TOK_DEV, 0)]
        grad_slab = lax.dynamic_slice_in_dim(grad_attended, start, TOK_DEV, 0)
        offsets = []
        for level in range(LEVELS):
            other = (((slab >> level) ^ 1) * BLOCK).astype(jnp.int32)
            offsets.append(other)
            key_parts.append(lax.dynamic_slice_in_dim(coarse_keys[level], other, BLOCK, 0))
            value_parts.append(lax.dynamic_slice_in_dim(coarse_values[level], other, BLOCK, 0))
        key_list = jnp.concatenate(key_parts, axis=0)
        value_list = jnp.concatenate(value_parts, axis=0)
        query_heads = query_slab.reshape(TOK_DEV, HEADS, HDIM).astype(jnp.float32)
        key_heads = key_list.reshape(list_rows, HEADS, HDIM).astype(jnp.float32)
        value_heads = value_list.reshape(list_rows, HEADS, HDIM).astype(jnp.float32)
        grad_heads = grad_slab.reshape(TOK_DEV, HEADS, HDIM).astype(jnp.float32)
        scores = jnp.einsum("thd,khd->htk", query_heads, key_heads) * inv_scale
        shifted = jnp.exp(scores - jnp.max(scores, axis=2, keepdims=True))
        probs = shifted / jnp.sum(shifted, axis=2, keepdims=True)
        probs_low = probs.astype(jnp.bfloat16).astype(jnp.float32)
        attended = jnp.einsum("htk,khd->thd", probs_low, value_heads).reshape(TOK_DEV, D).astype(jnp.bfloat16)
        prob_grad = jnp.einsum("thd,khd->htk", grad_heads, value_heads)
        centre = jnp.sum(probs * prob_grad, axis=2, keepdims=True)
        score_grad = (probs * (prob_grad - centre) * inv_scale).astype(jnp.bfloat16).astype(jnp.float32)
        query_grad = jnp.einsum("htk,khd->thd", score_grad, key_heads).reshape(TOK_DEV, D).astype(jnp.bfloat16)
        key_terms = jnp.einsum("htk,thd->khd", score_grad, query_heads).reshape(list_rows, D)
        value_terms = jnp.einsum("htk,thd->khd", probs_low, grad_heads).reshape(list_rows, D)
        new_keys = []
        new_values = []
        for level in range(LEVELS):
            first = TOK_DEV + level * BLOCK
            old_key = lax.dynamic_slice_in_dim(key_accum[level], offsets[level], BLOCK, 0)
            old_value = lax.dynamic_slice_in_dim(value_accum[level], offsets[level], BLOCK, 0)
            new_keys.append(lax.dynamic_update_slice_in_dim(key_accum[level], old_key + key_terms[first:first + BLOCK], offsets[level], 0))
            new_values.append(lax.dynamic_update_slice_in_dim(value_accum[level], old_value + value_terms[first:first + BLOCK], offsets[level], 0))
        return (new_keys, new_values), (attended, query_grad, key_terms[:TOK_DEV], value_terms[:TOK_DEV])

    start_keys = [jnp.zeros((TOKENS // run_lengths[level], D), jnp.float32) for level in range(LEVELS)]
    start_values = [jnp.zeros((TOKENS // run_lengths[level], D), jnp.float32) for level in range(LEVELS)]
    (key_accum, value_accum), stacked = lax.scan(slab_step, (start_keys, start_values), jnp.arange(SLABS, dtype=jnp.int32))
    attended = stacked[0].reshape(TOKENS, D)
    query_grad = stacked[1].reshape(TOKENS, D)
    key_sum = stacked[2].reshape(TOKENS, D)
    value_sum = stacked[3].reshape(TOKENS, D)
    for level in range(LEVELS):
        key_sum = key_sum + jnp.repeat(key_accum[level] / run_lengths[level], run_lengths[level], axis=0)
        value_sum = value_sum + jnp.repeat(value_accum[level], run_lengths[level], axis=0)
    output = jnp.dot(attended, out_weight.T, preferred_element_type=jnp.float32).astype(jnp.bfloat16)
    return output, query_grad, key_sum.astype(jnp.bfloat16), value_sum.astype(jnp.bfloat16)
```

```python
import functools
import math

import jax
import jax.numpy as jnp
from jax import lax
from jax.experimental import pallas as pl
from jax.experimental.pallas import tpu as pltpu
from jax.sharding import PartitionSpec as P

HDIM = 128
BLOCK = 128
RING = 4
MESH = pl.DeviceIdType.MESH
BF16 = jnp.bfloat16
F32 = jnp.float32


def dot(left, right, dims=((1,), (0,))):
    return lax.dot_general(left, right, (dims, ((), ())), preferred_element_type=F32)


def iota(shape, dim):
    return lax.broadcasted_iota(jnp.int32, shape, dim)


def arrive(buf, sem):
    pltpu.make_async_copy(buf, buf, sem).wait()


def kernel(
    units, q, k, v, w, og, out, dq, dk, dv,
    wv, ogv, dacc, dab, kg, vg, qg, ag, c01, e01, ck, cv, k6, c6, kf, vf, f6,
    gks, gvs, g6s, gkr, gvr, g6r, g1k, g1v, dkl, dvl, atb, dqb, dkb, dvb, atg, pob, por,
    local, sent, came,
):
    far = units.bit_length() - 1
    me = lax.axis_index("seq")
    core = lax.axis_index("head")
    other = 1 - core
    x = lax.rem(me, RING)
    unit = me // RING
    tokens = RING * BLOCK
    wide = q.shape[1] // RING
    inv_scale = 1.0 / math.sqrt(HDIM)

    def columns(i):
        return pl.ds(pl.multiple_of(i * wide, wide), wide)

    def ring_device(d):
        peer = lax.rem(x + d, RING)
        return peer, (unit * RING + peer, core)

    def send(src, dst, slot, device):
        pltpu.make_async_remote_copy(
            src_ref=src, dst_ref=dst, send_sem=sent.at[slot], recv_sem=came.at[slot],
            device_id=device, device_id_type=MESH,
        ).start()

    def scatter_cols(src, dst, slot):
        for d in range(1, RING):
            peer, device = ring_device(d)
            send(src.at[:, columns(peer)], dst.at[x], slot, device)
        pltpu.make_async_copy(src.at[:, columns(x)], dst.at[x], came.at[slot]).start()

    def gather_cols(src, dst, slot):
        for d in range(1, RING):
            peer, device = ring_device(d)
            send(src.at[peer], dst.at[:, columns(x)], slot, device)
        pltpu.make_async_copy(src.at[x], dst.at[:, columns(x)], came.at[slot]).start()

    def far_send(j, source, landing, slot):
        n = 1 << j
        group = unit // n
        base = (group + 1 - 2 * lax.rem(group, 2)) * n
        mine = lax.rem(unit, n)

        def one(i, carry):
            send(source(i), landing(mine), slot, ((base + i) * RING + x, core))
            return carry

        lax.fori_loop(0, n, one, 0)

    def rows_at(ref, j, i):
        rows = BLOCK >> j
        return ref.at[j, pl.ds(pl.multiple_of(i * rows, rows), rows)]

    own_w = pltpu.make_async_copy(
        w.at[pl.ds(pl.multiple_of(core * (w.shape[0] // 2), 128), w.shape[0] // 2)], wv.at[0], local.at[0]
    )
    other_w = pltpu.make_async_copy(
        w.at[pl.ds(pl.multiple_of(other * (w.shape[0] // 2), 128), w.shape[0] // 2)], wv.at[1], local.at[1]
    )
    own_og = pltpu.make_async_copy(og, ogv.at[0], local.at[2])
    own_og.start()
    own_w.start()
    other_w.start()

    barrier = pltpu.get_barrier_semaphore()
    pl.semaphore_signal(barrier, inc=1, device_id=(me, other), device_id_type=MESH)
    for d in range(1, RING):
        pl.semaphore_signal(barrier, inc=1, device_id=ring_device(d)[1], device_id_type=MESH)

    def greet(d, carry):
        there = lax.rem(unit + d, units)
        pl.semaphore_signal(barrier, inc=1, device_id=(there * RING + x, core), device_id_type=MESH)
        return carry

    lax.fori_loop(1, units, greet, 0)

    first = 0
    for level in range(1, far + 2):
        count = tokens >> level
        rows = max(count, 16)
        hit = (iota((rows, tokens), 1) >> level) == iota((rows, tokens), 0)
        c01[first : first + rows, :] = jnp.where(hit, 1.0, 0.0).astype(BF16)
        first += rows
    for j in range(far):
        shape = (tokens, BLOCK)
        hit = (iota(shape, 0) >> (j + 2)) == (iota(shape, 1) & ((BLOCK >> j) - 1))
        e01[:, j * BLOCK : (j + 1) * BLOCK] = jnp.where(hit, 1.0, 0.0).astype(BF16)
    shape = (tokens, 2 * BLOCK)
    hit = (iota(shape, 0) >> 1) == iota(shape, 1)
    e01[:, far * BLOCK : (far + 2) * BLOCK] = jnp.where(hit, 1.0, 0.0).astype(BF16)

    own_og.wait()
    own_w.wait()
    dacc[...] = dot(ogv[0], wv[0])

    pl.semaphore_wait(barrier, units - 1 + RING)

    send(ogv.at[0], ogv.at[1], 0, (me, other))
    scatter_cols(k, kg, 1)
    scatter_cols(v, vg, 2)
    scatter_cols(q, qg, 3)

    other_w.wait()
    arrive(ogv.at[1], came.at[0])
    dab[...] = (dacc[...] + dot(ogv[1], wv[1])).astype(BF16)
    scatter_cols(dab, ag, 4)

    starts = [2 * BLOCK]
    for j in range(far):
        starts.append(starts[-1] + (BLOCK >> j))
    arrive(kg, came.at[1])
    coarse = dot(c01[2 * BLOCK :, :], kg[...].reshape(tokens, wide))
    for j in range(far - 1):
        low = starts[j] - 2 * BLOCK
        ck[starts[j] : starts[j + 1], :] = (coarse[low : low + (BLOCK >> j)] * (1.0 / (4 << j))).astype(BF16)
        far_send(j, lambda i: ck.at[starts[j] : starts[j + 1]], lambda i: rows_at(kf, j, i), 5 + j)
    low = starts[far - 1] - 2 * BLOCK
    k6[...] = coarse[low : low + 8] * (1.0 / (4 << (far - 1)))
    arrive(vg, came.at[2])
    coarse = dot(c01[2 * BLOCK :, :], vg[...].reshape(tokens, wide))
    for j in range(far - 1):
        low = starts[j] - 2 * BLOCK
        cv[starts[j] : starts[j + 1], :] = coarse[low : low + (BLOCK >> j)].astype(BF16)
        far_send(j, lambda i: cv.at[starts[j] : starts[j + 1]], lambda i: rows_at(vf, j, i), 9 + j)
    low = starts[far - 1] - 2 * BLOCK
    c6[...] = jnp.concatenate([k6[...], coarse[low : low + 8]], axis=0).astype(BF16)
    far_send(far - 1, lambda i: c6, lambda i: f6.at[i], 13)
    ck[: 2 * BLOCK, :] = (dot(c01[: 2 * BLOCK, :], kg[...].reshape(tokens, wide)) * 0.5).astype(BF16)
    cv[: 2 * BLOCK, :] = dot(c01[: 2 * BLOCK, :], vg[...].reshape(tokens, wide)).astype(BF16)

    arrive(qg, came.at[3])
    arrive(ag, came.at[4])
    for j in range(far - 1):
        arrive(kf.at[j], came.at[5 + j])
        arrive(vf.at[j], came.at[9 + j])
    arrive(f6, came.at[13])
    mixed = f6[...].astype(F32)
    kf[far - 1] = mixed[:, :8].reshape(BLOCK, wide).astype(BF16)
    vf[far - 1] = mixed[:, 8:].reshape(BLOCK, wide).astype(BF16)

    pair = 2 * BLOCK

    def one_head(h, carry):
        cols = pl.ds(pl.multiple_of(h * HDIM, HDIM), HDIM)
        far_k = kf[:, :, cols].reshape(far * BLOCK, HDIM)
        far_v = vf[:, :, cols].reshape(far * BLOCK, HDIM)
        sum_k = None
        sum_v = None
        for p in range(RING // 2):
            there = 1 - p
            qp = qg[2 * p : 2 * p + 2, :, cols].reshape(pair, HDIM)
            ap = ag[2 * p : 2 * p + 2, :, cols].reshape(pair, HDIM)
            keys = jnp.concatenate(
                [
                    kg[2 * p : 2 * p + 2, :, cols].reshape(pair, HDIM),
                    ck[there * BLOCK : (there + 1) * BLOCK, cols],
                    far_k,
                ],
                axis=0,
            )
            values = jnp.concatenate(
                [
                    vg[2 * p : 2 * p + 2, :, cols].reshape(pair, HDIM),
                    cv[there * BLOCK : (there + 1) * BLOCK, cols],
                    far_v,
                ],
                axis=0,
            )
            scores = dot(keys, qp, ((1,), (1,))) * inv_scale
            shifted = jnp.exp(scores - jnp.max(scores, axis=0, keepdims=True))
            prob = shifted * (1.0 / jnp.sum(shifted, axis=0, keepdims=True))
            prob_low = prob.astype(BF16)
            prob_grad = dot(values, ap, ((1,), (1,)))
            centre = jnp.sum(prob * prob_grad, axis=0, keepdims=True)
            score_grad = (prob * (prob_grad - centre) * inv_scale).astype(BF16)
            attended = dot(values, prob_low, ((0,), (0,))).T
            query_grad = dot(keys, score_grad, ((0,), (0,))).T
            key_terms = dot(score_grad, qp)
            value_terms = dot(prob_low, ap)
            for s in range(2):
                rows = slice(s * BLOCK, (s + 1) * BLOCK)
                atb[2 * p + s, :, cols] = attended[rows].astype(BF16)
                dqb[2 * p + s, :, cols] = query_grad[rows].astype(BF16)
            dkl[p * pair : (p + 1) * pair, cols] = key_terms[:pair]
            dvl[p * pair : (p + 1) * pair, cols] = value_terms[:pair]
            near = slice(there * BLOCK, (there + 1) * BLOCK)
            g1k[near, cols] = key_terms[pair : pair + BLOCK].astype(BF16)
            g1v[near, cols] = value_terms[pair : pair + BLOCK].astype(BF16)
            far_terms = key_terms[pair + BLOCK :]
            sum_k = far_terms if sum_k is None else sum_k + far_terms
            far_terms = value_terms[pair + BLOCK :]
            sum_v = far_terms if sum_v is None else sum_v + far_terms
        last = (far - 1) * BLOCK
        gks[:, :, cols] = sum_k[:last].astype(BF16).reshape(far - 1, BLOCK, HDIM)
        gvs[:, :, cols] = sum_v[:last].astype(BF16).reshape(far - 1, BLOCK, HDIM)
        both = jnp.concatenate(
            [sum_k[last:].reshape(16, 8, HDIM), sum_v[last:].reshape(16, 8, HDIM)], axis=1
        )
        g6s[:, :, cols] = both.astype(BF16)
        return carry

    lax.fori_loop(0, wide // HDIM, one_head, 0)

    for j in range(far - 1):
        far_send(j, lambda i: rows_at(gks, j, i), lambda i: rows_at(gkr, j, i), 14 + j)
    far_send(far - 1, lambda i: g6s.at[i], lambda i: g6r.at[i], 22)
    for j in range(far - 1):
        far_send(j, lambda i: rows_at(gvs, j, i), lambda i: rows_at(gvr, j, i), 18 + j)
    gather_cols(atb, atg, 23)
    gather_cols(dqb, dq, 24)

    arrive(atg, came.at[23])
    pob[...] = dot(atg[...], wv[1], ((1,), (1,))).astype(BF16)
    send(pob, por, 27, (me, other))
    own_out = dot(atg[...], wv[0], ((1,), (1,)))
    arrive(por, came.at[27])
    pob2 = (own_out + por[...].astype(F32)).astype(BF16)
    atg[...] = pob2
    write_out = pltpu.make_async_copy(atg, out, local.at[3])
    write_out.start()

    def spread(received, near, local_sum, mean):
        total = local_sum[...]
        pieces = []
        for j, piece in enumerate(received):
            pieces.append(piece * (1.0 / (4 << j)) if mean else piece)
        piece = near[...].astype(F32)
        pieces.append(piece * 0.5 if mean else piece)
        packed = jnp.concatenate([piece.astype(BF16) for piece in pieces], axis=0)
        total = total + dot(e01[...], packed)
        return total.astype(BF16).reshape(RING, BLOCK, wide)

    for j in range(far - 1):
        arrive(gkr.at[j], came.at[14 + j])
    arrive(g6r, came.at[22])
    mixed = g6r[...].astype(F32)
    received = [gkr[j].astype(F32) for j in range(far - 1)] + [mixed[:, :8].reshape(BLOCK, wide)]
    dkb[...] = spread(received, g1k, dkl, True)
    gather_cols(dkb, dk, 25)
    for j in range(far - 1):
        arrive(gvr.at[j], came.at[18 + j])
    received = [gvr[j].astype(F32) for j in range(far - 1)] + [mixed[:, 8:].reshape(BLOCK, wide)]
    dvb[...] = spread(received, g1v, dvl, False)
    gather_cols(dvb, dv, 26)

    arrive(ogv.at[0], sent.at[0])
    for slot, buf in ((1, kg), (2, vg), (3, qg), (4, ag), (23, atb), (24, dqb), (25, dkb), (26, dvb)):
        arrive(buf.at[: RING - 1], sent.at[slot])
    for j in range(far - 1):
        for slot in (5, 9, 14, 18):
            arrive(kf.at[j], sent.at[slot + j])
    arrive(f6, sent.at[13])
    arrive(g6r, sent.at[22])
    arrive(pob, sent.at[27])
    arrive(dq, came.at[24])
    arrive(dk, came.at[25])
    arrive(dv, came.at[26])
    write_out.wait()


def on_device(queries, key_tokens, value_tokens, out_weight, output_grad):
    seq_count = lax.axis_size("seq")
    units = seq_count // RING
    far = units.bit_length() - 1
    rows, width = queries.shape
    wide = width // RING
    tokens = RING * rows
    quarter = (RING, BLOCK, wide)
    vm = pltpu.VMEM
    scratch = [
        vm((2, width, width), BF16), vm((2, rows, width), BF16), vm((rows, width), F32), vm((rows, width), BF16),
        vm(quarter, BF16), vm(quarter, BF16), vm(quarter, BF16), vm(quarter, BF16),
        vm((tokens, tokens), BF16), vm((tokens, (far + 2) * BLOCK), BF16),
        vm((tokens, wide), BF16), vm((tokens, wide), BF16), vm((8, wide), F32), vm((16, wide), BF16),
        vm((far, BLOCK, wide), BF16), vm((far, BLOCK, wide), BF16), vm((16, 16, wide), BF16),
        vm((far - 1, BLOCK, wide), BF16), vm((far - 1, BLOCK, wide), BF16), vm((16, 16, wide), BF16),
        vm((far - 1, BLOCK, wide), BF16), vm((far - 1, BLOCK, wide), BF16), vm((16, 16, wide), BF16),
        vm((2 * BLOCK, wide), BF16), vm((2 * BLOCK, wide), BF16), vm((tokens, wide), F32), vm((tokens, wide), F32),
        vm(quarter, BF16), vm(quarter, BF16), vm(quarter, BF16), vm(quarter, BF16),
        vm((rows, width), BF16), vm((rows, width), BF16), vm((rows, width), BF16),
        pltpu.SemaphoreType.DMA((4,)), pltpu.SemaphoreType.DMA((28,)), pltpu.SemaphoreType.DMA((28,)),
    ]
    anywhere = pl.BlockSpec(memory_space=pl.ANY)
    return pl.pallas_call(
        functools.partial(kernel, units),
        out_shape=[jax.ShapeDtypeStruct((rows, width), BF16)] * 4,
        in_specs=[anywhere] * 5,
        out_specs=[anywhere] * 4,
        scratch_shapes=scratch,
        compiler_params=pltpu.CompilerParams(
            collective_id=0, has_side_effects=True, vmem_limit_bytes=60 * 1024 * 1024
        ),
        name="layer",
    )(queries, key_tokens, value_tokens, out_weight, output_grad)


def solution(mesh):
    placed = (P("seq", "head"), P("seq", "head"), P("seq", "head"), P(None, "head"), P("seq", "head"))
    return jax.shard_map(
        on_device,
        mesh=mesh,
        in_specs=placed,
        out_specs=(P("seq", "head"),) * 4,
        check_vma=False,
    )
```

```python
import functools
import math

import jax
import jax.numpy as jnp
from jax import lax
from jax.experimental import pallas as pl
from jax.experimental.pallas import tpu as pltpu
from jax.sharding import PartitionSpec as P

HDIM = 128
BLOCK = 128
RING = 4
SLOTS = 28
MESH = pl.DeviceIdType.MESH
BF16 = jnp.bfloat16
F32 = jnp.float32


def dot(left, right, dims=((1,), (0,))):
    return lax.dot_general(left, right, (dims, ((), ())), preferred_element_type=F32)


def iota(shape, dim):
    return lax.broadcasted_iota(jnp.int32, shape, dim)


def arrive(buf, sem):
    pltpu.make_async_copy(buf, buf, sem).wait()


def kernel(
    units, q, k, v, w, og, out, dq, dk, dv,
    wv, ogv, dacc, dab, kg, vg, qg, ag, c01, e01, ck, cv, k6, c6, kf, vf, f6,
    gks, gvs, g6s, gkr, gvr, g6r, g1k, g1v, dkl, dvl, atb, dqb, dkb, dvb, atg, pob, por, pob2,
    local, sent, came,
):
    far = units.bit_length() - 1
    me = lax.axis_index("seq")
    core = lax.axis_index("head")
    other = 1 - core
    x = lax.rem(me, RING)
    unit = me // RING
    tokens = RING * BLOCK
    wide = q.shape[1] // RING
    inv_scale = 1.0 / math.sqrt(HDIM)

    def columns(i, h):
        return pl.ds(pl.multiple_of(i * wide + h * HDIM, HDIM), HDIM)

    def ring_device(d):
        peer = lax.rem(x + d, RING)
        return peer, (unit * RING + peer, core)

    def send(src, dst, sem, device):
        pltpu.make_async_remote_copy(
            src_ref=src, dst_ref=dst, send_sem=sent.at[sem], recv_sem=came.at[sem],
            device_id=device, device_id_type=MESH,
        ).start()

    def scatter_cols(src, dst, h, slot):
        for d in range(1, RING):
            peer, device = ring_device(d)
            send(src.at[:, columns(peer, h)], dst.at[h, x], h * SLOTS + slot, device)
        pltpu.make_async_copy(src.at[:, columns(x, h)], dst.at[h, x], came.at[h * SLOTS + slot]).start()

    def gather_cols(src, dst, h, slot):
        for d in range(1, RING):
            peer, device = ring_device(d)
            send(src.at[h, peer], dst.at[:, columns(x, h)], h * SLOTS + slot, device)
        pltpu.make_async_copy(src.at[h, x], dst.at[:, columns(x, h)], came.at[h * SLOTS + slot]).start()

    def far_send(j, source, landing, sem):
        n = 1 << j
        group = unit // n
        base = (group + 1 - 2 * lax.rem(group, 2)) * n
        mine = lax.rem(unit, n)

        def one(i, carry):
            send(source(i), landing(mine), sem, ((base + i) * RING + x, core))
            return carry

        lax.fori_loop(0, n, one, 0)

    def rows_at(ref, h, j, i):
        rows = BLOCK >> j
        return ref.at[h, j, pl.ds(pl.multiple_of(i * rows, rows), rows)]

    own_w = pltpu.make_async_copy(
        w.at[pl.ds(pl.multiple_of(core * (w.shape[0] // 2), 128), w.shape[0] // 2)], wv.at[0], local.at[0]
    )
    other_w = pltpu.make_async_copy(
        w.at[pl.ds(pl.multiple_of(other * (w.shape[0] // 2), 128), w.shape[0] // 2)], wv.at[1], local.at[1]
    )
    own_og = pltpu.make_async_copy(og, ogv.at[0], local.at[2])
    own_og.start()
    own_w.start()
    other_w.start()

    barrier = pltpu.get_barrier_semaphore()
    pl.semaphore_signal(barrier, inc=1, device_id=(me, other), device_id_type=MESH)
    for d in range(1, RING):
        pl.semaphore_signal(barrier, inc=1, device_id=ring_device(d)[1], device_id_type=MESH)

    def greet(d, carry):
        there = lax.rem(unit + d, units)
        pl.semaphore_signal(barrier, inc=1, device_id=(there * RING + x, core), device_id_type=MESH)
        return carry

    lax.fori_loop(1, units, greet, 0)

    first = 0
    for level in range(1, far + 2):
        count = tokens >> level
        rows = max(count, 16)
        hit = (iota((rows, tokens), 1) >> level) == iota((rows, tokens), 0)
        c01[first : first + rows, :] = jnp.where(hit, 1.0, 0.0).astype(BF16)
        first += rows
    for j in range(far):
        shape = (tokens, BLOCK)
        hit = (iota(shape, 0) >> (j + 2)) == (iota(shape, 1) & ((BLOCK >> j) - 1))
        e01[:, j * BLOCK : (j + 1) * BLOCK] = jnp.where(hit, 1.0, 0.0).astype(BF16)
    shape = (tokens, 2 * BLOCK)
    hit = (iota(shape, 0) >> 1) == iota(shape, 1)
    e01[:, far * BLOCK : (far + 2) * BLOCK] = jnp.where(hit, 1.0, 0.0).astype(BF16)

    own_og.wait()
    own_w.wait()
    dacc[...] = dot(ogv[0], wv[0])

    pl.semaphore_wait(barrier, units - 1 + RING)

    starts = [2 * BLOCK]
    for j in range(far):
        starts.append(starts[-1] + (BLOCK >> j))
    low6 = starts[far - 1] - 2 * BLOCK

    def coarse_keys(h):
        base = h * SLOTS
        arrive(kg.at[h], came.at[base + 1])
        coarse = dot(c01[2 * BLOCK :, :], kg[h].reshape(tokens, HDIM))
        for j in range(far - 1):
            low = starts[j] - 2 * BLOCK
            ck[h, starts[j] : starts[j + 1], :] = (coarse[low : low + (BLOCK >> j)] * (1.0 / (4 << j))).astype(BF16)
            far_send(j, lambda i: ck.at[h, starts[j] : starts[j + 1]], lambda i: rows_at(kf, h, j, i), base + 5 + j)
        k6[...] = coarse[low6 : low6 + 8] * (1.0 / (4 << (far - 1)))

    def coarse_values(h):
        base = h * SLOTS
        arrive(vg.at[h], came.at[base + 2])
        coarse = dot(c01[2 * BLOCK :, :], vg[h].reshape(tokens, HDIM))
        for j in range(far - 1):
            low = starts[j] - 2 * BLOCK
            cv[h, starts[j] : starts[j + 1], :] = coarse[low : low + (BLOCK >> j)].astype(BF16)
            far_send(j, lambda i: cv.at[h, starts[j] : starts[j + 1]], lambda i: rows_at(vf, h, j, i), base + 9 + j)
        c6[h] = jnp.concatenate([k6[...], coarse[low6 : low6 + 8]], axis=0).astype(BF16)
        far_send(far - 1, lambda i: c6.at[h], lambda i: f6.at[h, i], base + 13)

    def near_rows(h):
        ck[h, : 2 * BLOCK, :] = (dot(c01[: 2 * BLOCK, :], kg[h].reshape(tokens, HDIM)) * 0.5).astype(BF16)
        cv[h, : 2 * BLOCK, :] = dot(c01[: 2 * BLOCK, :], vg[h].reshape(tokens, HDIM)).astype(BF16)

    scatter_cols(k, kg, 0, 1)
    scatter_cols(v, vg, 0, 2)
    send(ogv.at[0], ogv.at[1], 0, (me, other))
    scatter_cols(q, qg, 0, 3)
    coarse_keys(0)
    coarse_values(0)
    other_w.wait()
    arrive(ogv.at[1], came.at[0])
    dab[...] = (dacc[...] + dot(ogv[1], wv[1])).astype(BF16)
    scatter_cols(dab, ag, 0, 4)
    scatter_cols(k, kg, 1, 1)
    scatter_cols(v, vg, 1, 2)
    scatter_cols(q, qg, 1, 3)
    scatter_cols(dab, ag, 1, 4)
    near_rows(0)
    coarse_keys(1)
    coarse_values(1)
    near_rows(1)

    pair = 2 * BLOCK
    last = (far - 1) * BLOCK

    def one_head(h):
        base = h * SLOTS
        arrive(qg.at[h], came.at[base + 3])
        arrive(ag.at[h], came.at[base + 4])
        for j in range(far - 1):
            arrive(kf.at[h, j], came.at[base + 5 + j])
            arrive(vf.at[h, j], came.at[base + 9 + j])
        arrive(f6.at[h], came.at[base + 13])
        mixed = f6[h].astype(F32)
        kf[h, far - 1] = mixed[:, :8].reshape(BLOCK, HDIM).astype(BF16)
        vf[h, far - 1] = mixed[:, 8:].reshape(BLOCK, HDIM).astype(BF16)
        far_k = kf[h].reshape(far * BLOCK, HDIM)
        far_v = vf[h].reshape(far * BLOCK, HDIM)
        sum_k = None
        sum_v = None
        for p in range(RING // 2):
            there = 1 - p
            near = slice(there * BLOCK, (there + 1) * BLOCK)
            two = slice(2 * p, 2 * p + 2)
            qp = qg[h, two].reshape(pair, HDIM)
            ap = ag[h, two].reshape(pair, HDIM)
            keys = jnp.concatenate([kg[h, two].reshape(pair, HDIM), ck[h, near, :], far_k], axis=0)
            values = jnp.concatenate([vg[h, two].reshape(pair, HDIM), cv[h, near, :], far_v], axis=0)
            scores = dot(keys, qp, ((1,), (1,))) * inv_scale
            shifted = jnp.exp(scores - jnp.max(scores, axis=0, keepdims=True))
            prob = shifted * (1.0 / jnp.sum(shifted, axis=0, keepdims=True))
            prob_low = prob.astype(BF16)
            prob_grad = dot(values, ap, ((1,), (1,)))
            centre = jnp.sum(prob * prob_grad, axis=0, keepdims=True)
            score_grad = (prob * (prob_grad - centre) * inv_scale).astype(BF16)
            attended = dot(values, prob_low, ((0,), (0,))).T
            query_grad = dot(keys, score_grad, ((0,), (0,))).T
            key_terms = dot(score_grad, qp)
            value_terms = dot(prob_low, ap)
            for s in range(2):
                rows = slice(s * BLOCK, (s + 1) * BLOCK)
                atb[h, 2 * p + s] = attended[rows].astype(BF16)
                dqb[h, 2 * p + s] = query_grad[rows].astype(BF16)
            dkl[h, p * pair : (p + 1) * pair, :] = key_terms[:pair]
            dvl[h, p * pair : (p + 1) * pair, :] = value_terms[:pair]
            g1k[h, near, :] = key_terms[pair : pair + BLOCK].astype(BF16)
            g1v[h, near, :] = value_terms[pair : pair + BLOCK].astype(BF16)
            far_terms = key_terms[pair + BLOCK :]
            sum_k = far_terms if sum_k is None else sum_k + far_terms
            far_terms = value_terms[pair + BLOCK :]
            sum_v = far_terms if sum_v is None else sum_v + far_terms
        gks[h] = sum_k[:last].astype(BF16).reshape(far - 1, BLOCK, HDIM)
        gvs[h] = sum_v[:last].astype(BF16).reshape(far - 1, BLOCK, HDIM)
        both = jnp.concatenate(
            [sum_k[last:].reshape(16, 8, HDIM), sum_v[last:].reshape(16, 8, HDIM)], axis=1
        )
        g6s[h] = both.astype(BF16)
        for j in range(far - 1):
            far_send(j, lambda i: rows_at(gks, h, j, i), lambda i: rows_at(gkr, h, j, i), base + 14 + j)
        far_send(far - 1, lambda i: g6s.at[h, i], lambda i: g6r.at[h, i], base + 22)
        for j in range(far - 1):
            far_send(j, lambda i: rows_at(gvs, h, j, i), lambda i: rows_at(gvr, h, j, i), base + 18 + j)
        gather_cols(atb, atg, h, 23)
        gather_cols(dqb, dq, h, 24)

    def spread(h, received, near, local_sum, mean):
        pieces = []
        for j, piece in enumerate(received):
            pieces.append(piece * (1.0 / (4 << j)) if mean else piece)
        piece = near[h].astype(F32)
        pieces.append(piece * 0.5 if mean else piece)
        packed = jnp.concatenate([piece.astype(BF16) for piece in pieces], axis=0)
        total = local_sum[h] + dot(e01[...], packed)
        return total.astype(BF16).reshape(RING, BLOCK, HDIM)

    def key_grads(h):
        base = h * SLOTS
        for j in range(far - 1):
            arrive(gkr.at[h, j], came.at[base + 14 + j])
        arrive(g6r.at[h], came.at[base + 22])
        mixed = g6r[h].astype(F32)[:, :8].reshape(BLOCK, HDIM)
        received = [gkr[h, j].astype(F32) for j in range(far - 1)] + [mixed]
        dkb[h] = spread(h, received, g1k, dkl, True)
        gather_cols(dkb, dk, h, 25)

    def value_grads(h):
        base = h * SLOTS
        for j in range(far - 1):
            arrive(gvr.at[h, j], came.at[base + 18 + j])
        mixed = g6r[h].astype(F32)[:, 8:].reshape(BLOCK, HDIM)
        received = [gvr[h, j].astype(F32) for j in range(far - 1)] + [mixed]
        dvb[h] = spread(h, received, g1v, dvl, False)
        gather_cols(dvb, dv, h, 26)

    one_head(0)
    one_head(1)
    key_grads(0)
    value_grads(0)

    for h in range(2):
        arrive(atb.at[h], came.at[h * SLOTS + 23])
    pob[...] = dot(atg[...], wv[1], ((1,), (1,))).astype(BF16)
    send(pob, por, 27, (me, other))
    own_out = dot(atg[...], wv[0], ((1,), (1,)))
    arrive(por, came.at[27])
    pob2[...] = (own_out + por[...].astype(F32)).astype(BF16)
    write_out = pltpu.make_async_copy(pob2, out, local.at[3])
    write_out.start()

    key_grads(1)
    value_grads(1)

    arrive(ogv.at[0], sent.at[0])
    for h in range(2):
        base = h * SLOTS
        for slot, buf in ((1, kg), (2, vg), (3, qg), (4, ag), (23, atb), (24, dqb), (25, dkb), (26, dvb)):
            arrive(buf.at[h, : RING - 1], sent.at[base + slot])
        for j in range(far - 1):
            for slot in (5, 9, 14, 18):
                arrive(kf.at[h, j], sent.at[base + slot + j])
        arrive(f6.at[h], sent.at[base + 13])
        arrive(g6r.at[h], sent.at[base + 22])
        arrive(dqb.at[h], came.at[base + 24])
        arrive(dkb.at[h], came.at[base + 25])
        arrive(dvb.at[h], came.at[base + 26])
    arrive(pob, sent.at[27])
    write_out.wait()


def finish(a, b, c, d, ao, bo, co, do, buf, came, left):
    pairs = ((a, ao), (b, bo), (c, co), (d, do))
    loads = [pltpu.make_async_copy(src, buf.at[i], came.at[i]) for i, (src, _) in enumerate(pairs)]
    stores = [pltpu.make_async_copy(buf.at[i], dst, left.at[i]) for i, (_, dst) in enumerate(pairs)]
    for load in loads:
        load.start()
    for load, store in zip(loads, stores):
        load.wait()
        store.start()
    for store in stores:
        store.wait()


def on_device(queries, key_tokens, value_tokens, out_weight, output_grad):
    seq_count = lax.axis_size("seq")
    units = seq_count // RING
    far = units.bit_length() - 1
    rows, width = queries.shape
    wide = width // RING
    tokens = RING * rows
    quarter = (2, RING, BLOCK, HDIM)
    levels = (2, far - 1, BLOCK, HDIM)
    vm = pltpu.VMEM
    scratch = [
        vm((2, width, width), BF16), vm((2, rows, width), BF16), vm((rows, width), F32), vm((rows, width), BF16),
        vm(quarter, BF16), vm(quarter, BF16), vm(quarter, BF16), vm(quarter, BF16),
        vm((tokens, tokens), BF16), vm((tokens, (far + 2) * BLOCK), BF16),
        vm((2, tokens, HDIM), BF16), vm((2, tokens, HDIM), BF16), vm((8, HDIM), F32), vm((2, 16, HDIM), BF16),
        vm((2, far, BLOCK, HDIM), BF16), vm((2, far, BLOCK, HDIM), BF16), vm((2, 16, 16, HDIM), BF16),
        vm(levels, BF16), vm(levels, BF16), vm((2, 16, 16, HDIM), BF16),
        vm(levels, BF16), vm(levels, BF16), vm((2, 16, 16, HDIM), BF16),
        vm((2, 2 * BLOCK, HDIM), BF16), vm((2, 2 * BLOCK, HDIM), BF16),
        vm((2, tokens, HDIM), F32), vm((2, tokens, HDIM), F32),
        vm(quarter, BF16), vm(quarter, BF16), vm(quarter, BF16), vm(quarter, BF16),
        vm((rows, width), BF16), vm((rows, width), BF16), vm((rows, width), BF16), vm((rows, width), BF16),
        pltpu.SemaphoreType.DMA((4,)), pltpu.SemaphoreType.DMA((2 * SLOTS,)), pltpu.SemaphoreType.DMA((2 * SLOTS,)),
    ]
    anywhere = pl.BlockSpec(memory_space=pl.ANY)
    shapes = [jax.ShapeDtypeStruct((rows, width), BF16)] * 4
    results = pl.pallas_call(
        functools.partial(kernel, units),
        out_shape=shapes,
        in_specs=[anywhere] * 5,
        out_specs=[anywhere] * 4,
        scratch_shapes=scratch,
        compiler_params=pltpu.CompilerParams(
            collective_id=0, has_side_effects=True, vmem_limit_bytes=60 * 1024 * 1024
        ),
        name="layer",
    )(queries, key_tokens, value_tokens, out_weight, output_grad)
    return pl.pallas_call(
        finish,
        out_shape=shapes,
        in_specs=[anywhere] * 4,
        out_specs=[anywhere] * 4,
        scratch_shapes=[
            vm((4, rows, width), BF16), pltpu.SemaphoreType.DMA((4,)), pltpu.SemaphoreType.DMA((4,)),
        ],
        name="finish",
    )(*results)


def solution(mesh):
    placed = (P("seq", "head"), P("seq", "head"), P("seq", "head"), P(None, "head"), P("seq", "head"))
    return jax.shard_map(
        on_device,
        mesh=mesh,
        in_specs=placed,
        out_specs=(P("seq", "head"),) * 4,
        check_vma=False,
    )
```

```python
import functools
import math

import jax
import jax.numpy as jnp
from jax import lax
from jax.experimental import pallas as pl
from jax.experimental.pallas import tpu as pltpu
from jax.sharding import PartitionSpec as P

HDIM = 128
BLOCK = 128
RING = 4
SLOTS = 30
MESH = pl.DeviceIdType.MESH
BF16 = jnp.bfloat16
F32 = jnp.float32


def dot(left, right, dims=((1,), (0,))):
    return lax.dot_general(left, right, (dims, ((), ())), preferred_element_type=F32)


def iota(shape, dim):
    return lax.broadcasted_iota(jnp.int32, shape, dim)


def arrive(buf, sem):
    pltpu.make_async_copy(buf, buf, sem).wait()


def kernel(
    units, q, k, v, w, og, out, dq, dk, dv,
    wv, ogv, dacc, dab, kg, vg, qg, ag, c01, e01, ck, cv, k6, c6, kf, vf, f6,
    gks, gvs, g6s, gkr, gvr, g6r, g6m, g6c, g1k, g1v, dkl, dvl, atb, dqb, dkb, dvb, atg, pob, por, pob2,
    local, sent, came,
):
    far = units.bit_length() - 1
    me = lax.axis_index("seq")
    core = lax.axis_index("head")
    other = 1 - core
    x = lax.rem(me, RING)
    unit = me // RING
    tokens = RING * BLOCK
    wide = q.shape[1] // RING
    inv_scale = 1.0 / math.sqrt(HDIM)

    def columns(i, h):
        return pl.ds(pl.multiple_of(i * wide + h * HDIM, HDIM), HDIM)

    def ring_device(d):
        peer = lax.rem(x + d, RING)
        return peer, (unit * RING + peer, core)

    def send(src, dst, sem, device):
        pltpu.make_async_remote_copy(
            src_ref=src, dst_ref=dst, send_sem=sent.at[sem], recv_sem=came.at[sem],
            device_id=device, device_id_type=MESH,
        ).start()

    def scatter_cols(src, dst, h, slot):
        for d in range(1, RING):
            peer, device = ring_device(d)
            send(src.at[:, columns(peer, h)], dst.at[h, x], h * SLOTS + slot, device)
        pltpu.make_async_copy(src.at[:, columns(x, h)], dst.at[h, x], came.at[h * SLOTS + slot]).start()

    def gather_cols(src, dst, h, slot):
        for d in range(1, RING):
            peer, device = ring_device(d)
            send(src.at[h, peer], dst.at[:, columns(x, h)], h * SLOTS + slot, device)
        pltpu.make_async_copy(src.at[h, x], dst.at[:, columns(x, h)], came.at[h * SLOTS + slot]).start()

    def far_send(j, source, landing, sem):
        n = 1 << j
        group = unit // n
        base = (group + 1 - 2 * lax.rem(group, 2)) * n
        mine = lax.rem(unit, n)

        def one(i, carry):
            send(source(i), landing(mine), sem, ((base + i) * RING + x, core))
            return carry

        lax.fori_loop(0, n, one, 0)

    line = units // RING
    row = unit // line
    place = lax.rem(unit, line)
    mate = (((row + 1 - 2 * lax.rem(row, 2)) * line + place) * RING + x, core)

    def top_send(source, landing, sem):
        def one(i, carry):
            send(source(i), landing, sem, (((RING - 1 - row) * line + i) * RING + x, core))
            return carry

        lax.fori_loop(0, line, one, 0)

    def rows_at(ref, h, j, i):
        rows = BLOCK >> j
        return ref.at[h, j, pl.ds(pl.multiple_of(i * rows, rows), rows)]

    own_w = pltpu.make_async_copy(
        w.at[pl.ds(pl.multiple_of(core * (w.shape[0] // 2), 128), w.shape[0] // 2)], wv.at[0], local.at[0]
    )
    other_w = pltpu.make_async_copy(
        w.at[pl.ds(pl.multiple_of(other * (w.shape[0] // 2), 128), w.shape[0] // 2)], wv.at[1], local.at[1]
    )
    own_og = pltpu.make_async_copy(og, ogv.at[0], local.at[2])
    own_og.start()
    own_w.start()
    other_w.start()

    barrier = pltpu.get_barrier_semaphore()
    pl.semaphore_signal(barrier, inc=1, device_id=(me, other), device_id_type=MESH)
    for d in range(1, RING):
        pl.semaphore_signal(barrier, inc=1, device_id=ring_device(d)[1], device_id_type=MESH)

    def greet(d, carry):
        there = lax.rem(unit + d, units)
        pl.semaphore_signal(barrier, inc=1, device_id=(there * RING + x, core), device_id_type=MESH)
        return carry

    lax.fori_loop(1, units, greet, 0)

    first = 0
    for level in range(1, far + 2):
        count = tokens >> level
        rows = max(count, 16)
        hit = (iota((rows, tokens), 1) >> level) == iota((rows, tokens), 0)
        c01[first : first + rows, :] = jnp.where(hit, 1.0, 0.0).astype(BF16)
        first += rows
    for j in range(far):
        shape = (tokens, BLOCK)
        hit = (iota(shape, 0) >> (j + 2)) == (iota(shape, 1) & ((BLOCK >> j) - 1))
        e01[:, j * BLOCK : (j + 1) * BLOCK] = jnp.where(hit, 1.0, 0.0).astype(BF16)
    shape = (tokens, 2 * BLOCK)
    hit = (iota(shape, 0) >> 1) == iota(shape, 1)
    e01[:, far * BLOCK : (far + 2) * BLOCK] = jnp.where(hit, 1.0, 0.0).astype(BF16)

    own_og.wait()
    own_w.wait()
    dacc[...] = dot(ogv[0], wv[0])

    pl.semaphore_wait(barrier, units - 1 + RING)

    starts = [2 * BLOCK]
    for j in range(far):
        starts.append(starts[-1] + (BLOCK >> j))
    low6 = starts[far - 1] - 2 * BLOCK

    def coarse_keys(h):
        base = h * SLOTS
        arrive(kg.at[h], came.at[base + 1])
        coarse = dot(c01[2 * BLOCK :, :], kg[h].reshape(tokens, HDIM))
        for j in range(far - 1):
            low = starts[j] - 2 * BLOCK
            ck[h, starts[j] : starts[j + 1], :] = (coarse[low : low + (BLOCK >> j)] * (1.0 / (4 << j))).astype(BF16)
            far_send(j, lambda i: ck.at[h, starts[j] : starts[j + 1]], lambda i: rows_at(kf, h, j, i), base + 5 + j)
        k6[...] = coarse[low6 : low6 + 8] * (1.0 / (4 << (far - 1)))

    def coarse_values(h):
        base = h * SLOTS
        arrive(vg.at[h], came.at[base + 2])
        coarse = dot(c01[2 * BLOCK :, :], vg[h].reshape(tokens, HDIM))
        c6[h] = jnp.concatenate([k6[...], coarse[low6 : low6 + 8]], axis=0).astype(BF16)
        top_send(lambda i: c6.at[h], f6.at[h, 0, place], base + 13)
        for j in range(far - 1):
            low = starts[j] - 2 * BLOCK
            cv[h, starts[j] : starts[j + 1], :] = coarse[low : low + (BLOCK >> j)].astype(BF16)
            far_send(j, lambda i: cv.at[h, starts[j] : starts[j + 1]], lambda i: rows_at(vf, h, j, i), base + 9 + j)

    def top_forward(h):
        arrive(f6.at[h, 0], came.at[h * SLOTS + 13])
        send(f6.at[h, 0], f6.at[h, 1], h * SLOTS + 28, mate)

    def top_collect(h):
        arrive(g6m.at[h], came.at[h * SLOTS + 29])
        g6c[h] = (g6s[h, 0].astype(F32) + g6m[h].astype(F32)).astype(BF16)
        top_send(lambda i: g6c.at[h, i], g6r.at[h, place], h * SLOTS + 22)

    def near_rows(h):
        ck[h, : 2 * BLOCK, :] = (dot(c01[: 2 * BLOCK, :], kg[h].reshape(tokens, HDIM)) * 0.5).astype(BF16)
        cv[h, : 2 * BLOCK, :] = dot(c01[: 2 * BLOCK, :], vg[h].reshape(tokens, HDIM)).astype(BF16)

    scatter_cols(k, kg, 0, 1)
    scatter_cols(v, vg, 0, 2)
    send(ogv.at[0], ogv.at[1], 0, (me, other))
    scatter_cols(q, qg, 0, 3)
    coarse_keys(0)
    coarse_values(0)
    other_w.wait()
    arrive(ogv.at[1], came.at[0])
    dab[...] = (dacc[...] + dot(ogv[1], wv[1])).astype(BF16)
    scatter_cols(dab, ag, 0, 4)
    scatter_cols(k, kg, 1, 1)
    scatter_cols(v, vg, 1, 2)
    scatter_cols(q, qg, 1, 3)
    scatter_cols(dab, ag, 1, 4)
    near_rows(0)
    coarse_keys(1)
    top_forward(0)
    coarse_values(1)
    near_rows(1)

    pair = 2 * BLOCK
    last = (far - 1) * BLOCK

    def one_head(h):
        base = h * SLOTS
        arrive(qg.at[h], came.at[base + 3])
        arrive(ag.at[h], came.at[base + 4])
        for j in range(far - 1):
            arrive(kf.at[h, j], came.at[base + 5 + j])
            arrive(vf.at[h, j], came.at[base + 9 + j])
        arrive(f6.at[h, 1], came.at[base + 28])
        mixed = f6[h].reshape(2 * line, 16, HDIM).astype(F32)
        kf[h, far - 1] = mixed[:, :8].reshape(BLOCK, HDIM).astype(BF16)
        vf[h, far - 1] = mixed[:, 8:].reshape(BLOCK, HDIM).astype(BF16)
        far_k = kf[h].reshape(far * BLOCK, HDIM)
        far_v = vf[h].reshape(far * BLOCK, HDIM)
        sum_k = None
        sum_v = None
        for p in range(RING // 2):
            there = 1 - p
            near = slice(there * BLOCK, (there + 1) * BLOCK)
            two = slice(2 * p, 2 * p + 2)
            qp = qg[h, two].reshape(pair, HDIM)
            ap = ag[h, two].reshape(pair, HDIM)
            keys = jnp.concatenate([kg[h, two].reshape(pair, HDIM), ck[h, near, :], far_k], axis=0)
            values = jnp.concatenate([vg[h, two].reshape(pair, HDIM), cv[h, near, :], far_v], axis=0)
            scores = dot(keys, qp, ((1,), (1,))) * inv_scale
            shifted = jnp.exp(scores - jnp.max(scores, axis=0, keepdims=True))
            prob = shifted * (1.0 / jnp.sum(shifted, axis=0, keepdims=True))
            prob_low = prob.astype(BF16)
            prob_grad = dot(values, ap, ((1,), (1,)))
            centre = jnp.sum(prob * prob_grad, axis=0, keepdims=True)
            score_grad = (prob * (prob_grad - centre) * inv_scale).astype(BF16)
            attended = dot(values, prob_low, ((0,), (0,))).T
            query_grad = dot(keys, score_grad, ((0,), (0,))).T
            key_terms = dot(score_grad, qp)
            value_terms = dot(prob_low, ap)
            for s in range(2):
                rows = slice(s * BLOCK, (s + 1) * BLOCK)
                atb[h, 2 * p + s] = attended[rows].astype(BF16)
                dqb[h, 2 * p + s] = query_grad[rows].astype(BF16)
            dkl[h, p * pair : (p + 1) * pair, :] = key_terms[:pair]
            dvl[h, p * pair : (p + 1) * pair, :] = value_terms[:pair]
            g1k[h, near, :] = key_terms[pair : pair + BLOCK].astype(BF16)
            g1v[h, near, :] = value_terms[pair : pair + BLOCK].astype(BF16)
            far_terms = key_terms[pair + BLOCK :]
            sum_k = far_terms if sum_k is None else sum_k + far_terms
            far_terms = value_terms[pair + BLOCK :]
            sum_v = far_terms if sum_v is None else sum_v + far_terms
        gks[h] = sum_k[:last].astype(BF16).reshape(far - 1, BLOCK, HDIM)
        gvs[h] = sum_v[:last].astype(BF16).reshape(far - 1, BLOCK, HDIM)
        both = jnp.concatenate(
            [sum_k[last:].reshape(16, 8, HDIM), sum_v[last:].reshape(16, 8, HDIM)], axis=1
        )
        g6s[h] = both.astype(BF16).reshape(2, line, 16, HDIM)
        send(g6s.at[h, 1], g6m.at[h], base + 29, mate)
        for j in range(far - 1):
            far_send(j, lambda i: rows_at(gks, h, j, i), lambda i: rows_at(gkr, h, j, i), base + 14 + j)
        gather_cols(atb, atg, h, 23)
        gather_cols(dqb, dq, h, 24)
        if h == 0:
            top_forward(1)
        top_collect(h)
        for j in range(far - 1):
            far_send(j, lambda i: rows_at(gvs, h, j, i), lambda i: rows_at(gvr, h, j, i), base + 18 + j)

    def spread(h, received, near, local_sum, mean):
        pieces = []
        for j, piece in enumerate(received):
            pieces.append(piece * (1.0 / (4 << min(j, far - 1))) if mean else piece)
        piece = near[h].astype(F32)
        pieces.append(piece * 0.5 if mean else piece)
        packed = jnp.concatenate([piece.astype(BF16) for piece in pieces], axis=0)
        total = local_sum[h] + dot(e01[...], packed)
        return total.astype(BF16).reshape(RING, BLOCK, HDIM)

    def key_grads(h):
        base = h * SLOTS
        for j in range(far - 1):
            arrive(gkr.at[h, j], came.at[base + 14 + j])
        arrive(g6r.at[h], came.at[base + 22])
        mixed = g6r[h].astype(F32)[:, :8].reshape(line * 8, HDIM)
        received = [gkr[h, j].astype(F32) for j in range(far - 1)] + [mixed, jnp.zeros_like(mixed)]
        dkb[h] = spread(h, received, g1k, dkl, True)
        gather_cols(dkb, dk, h, 25)

    def value_grads(h):
        base = h * SLOTS
        for j in range(far - 1):
            arrive(gvr.at[h, j], came.at[base + 18 + j])
        mixed = g6r[h].astype(F32)[:, 8:].reshape(line * 8, HDIM)
        received = [gvr[h, j].astype(F32) for j in range(far - 1)] + [mixed, jnp.zeros_like(mixed)]
        dvb[h] = spread(h, received, g1v, dvl, False)
        gather_cols(dvb, dv, h, 26)

    one_head(0)
    one_head(1)
    key_grads(0)
    value_grads(0)

    for h in range(2):
        arrive(atb.at[h], came.at[h * SLOTS + 23])
    pob[...] = dot(atg[...], wv[1], ((1,), (1,))).astype(BF16)
    send(pob, por, 27, (me, other))
    own_out = dot(atg[...], wv[0], ((1,), (1,)))
    arrive(por, came.at[27])
    pob2[...] = (own_out + por[...].astype(F32)).astype(BF16)
    write_out = pltpu.make_async_copy(pob2, out, local.at[3])
    write_out.start()

    key_grads(1)
    value_grads(1)

    arrive(ogv.at[0], sent.at[0])
    for h in range(2):
        base = h * SLOTS
        for slot, buf in ((1, kg), (2, vg), (3, qg), (4, ag), (23, atb), (24, dqb), (25, dkb), (26, dvb)):
            arrive(buf.at[h, : RING - 1], sent.at[base + slot])
        for j in range(far - 1):
            for slot in (5, 9, 14, 18):
                arrive(kf.at[h, j], sent.at[base + slot + j])
        for slot in (13, 22, 28, 29):
            arrive(g6r.at[h], sent.at[base + slot])
        arrive(dqb.at[h], came.at[base + 24])
        arrive(dkb.at[h], came.at[base + 25])
        arrive(dvb.at[h], came.at[base + 26])
    arrive(pob, sent.at[27])
    write_out.wait()


def finish(a, b, c, d, ao, bo, co, do, buf, came, left):
    pairs = ((a, ao), (b, bo), (c, co), (d, do))
    loads = [pltpu.make_async_copy(src, buf.at[i], came.at[i]) for i, (src, _) in enumerate(pairs)]
    stores = [pltpu.make_async_copy(buf.at[i], dst, left.at[i]) for i, (_, dst) in enumerate(pairs)]
    for load in loads:
        load.start()
    for load, store in zip(loads, stores):
        load.wait()
        store.start()
    for store in stores:
        store.wait()


def on_device(queries, key_tokens, value_tokens, out_weight, output_grad):
    seq_count = lax.axis_size("seq")
    units = seq_count // RING
    far = units.bit_length() - 1
    rows, width = queries.shape
    wide = width // RING
    tokens = RING * rows
    quarter = (2, RING, BLOCK, HDIM)
    levels = (2, far - 1, BLOCK, HDIM)
    vm = pltpu.VMEM
    scratch = [
        vm((2, width, width), BF16), vm((2, rows, width), BF16), vm((rows, width), F32), vm((rows, width), BF16),
        vm(quarter, BF16), vm(quarter, BF16), vm(quarter, BF16), vm(quarter, BF16),
        vm((tokens, tokens), BF16), vm((tokens, (far + 2) * BLOCK), BF16),
        vm((2, tokens, HDIM), BF16), vm((2, tokens, HDIM), BF16), vm((8, HDIM), F32), vm((2, 16, HDIM), BF16),
        vm((2, far, BLOCK, HDIM), BF16), vm((2, far, BLOCK, HDIM), BF16), vm((2, 2, 8, 16, HDIM), BF16),
        vm(levels, BF16), vm(levels, BF16), vm((2, 2, 8, 16, HDIM), BF16),
        vm(levels, BF16), vm(levels, BF16), vm((2, 8, 16, HDIM), BF16),
        vm((2, 8, 16, HDIM), BF16), vm((2, 8, 16, HDIM), BF16),
        vm((2, 2 * BLOCK, HDIM), BF16), vm((2, 2 * BLOCK, HDIM), BF16),
        vm((2, tokens, HDIM), F32), vm((2, tokens, HDIM), F32),
        vm(quarter, BF16), vm(quarter, BF16), vm(quarter, BF16), vm(quarter, BF16),
        vm((rows, width), BF16), vm((rows, width), BF16), vm((rows, width), BF16), vm((rows, width), BF16),
        pltpu.SemaphoreType.DMA((4,)), pltpu.SemaphoreType.DMA((2 * SLOTS,)), pltpu.SemaphoreType.DMA((2 * SLOTS,)),
    ]
    anywhere = pl.BlockSpec(memory_space=pl.ANY)
    shapes = [jax.ShapeDtypeStruct((rows, width), BF16)] * 4
    results = pl.pallas_call(
        functools.partial(kernel, units),
        out_shape=shapes,
        in_specs=[anywhere] * 5,
        out_specs=[anywhere] * 4,
        scratch_shapes=scratch,
        compiler_params=pltpu.CompilerParams(
            collective_id=0, has_side_effects=True, vmem_limit_bytes=60 * 1024 * 1024
        ),
        name="layer",
    )(queries, key_tokens, value_tokens, out_weight, output_grad)
    return pl.pallas_call(
        finish,
        out_shape=shapes,
        in_specs=[anywhere] * 4,
        out_specs=[anywhere] * 4,
        scratch_shapes=[
            vm((4, rows, width), BF16), pltpu.SemaphoreType.DMA((4,)), pltpu.SemaphoreType.DMA((4,)),
        ],
        name="finish",
    )(*results)


def solution(mesh):
    placed = (P("seq", "head"), P("seq", "head"), P("seq", "head"), P(None, "head"), P("seq", "head"))
    return jax.shard_map(
        on_device,
        mesh=mesh,
        in_specs=placed,
        out_specs=(P("seq", "head"),) * 4,
        check_vma=False,
    )
```

```python
import functools
import math

import jax
import jax.numpy as jnp
from jax import lax
from jax.experimental import pallas as pl
from jax.experimental.pallas import tpu as pltpu
from jax.sharding import PartitionSpec as P

HDIM = 128
BLOCK = 128
RING = 4
SLOTS = 30
MESH = pl.DeviceIdType.MESH
BF16 = jnp.bfloat16
F32 = jnp.float32


def dot(left, right, dims=((1,), (0,))):
    return lax.dot_general(left, right, (dims, ((), ())), preferred_element_type=F32)


def iota(shape, dim):
    return lax.broadcasted_iota(jnp.int32, shape, dim)


def arrive(buf, sem):
    pltpu.make_async_copy(buf, buf, sem).wait()


def kernel(
    units, q, k, v, w, og, out, dq, dk, dv,
    wv, ogv, dacc, dab, kg, vg, qg, ag, c01, e01, ck, cv, k6, c6, kf, vf, f6,
    gks, gvs, g6s, gkr, gvr, g6r, g6m, g6c, g1k, g1v, dkl, dvl, atb, dqb, dkb, dvb, atg, pob, por, pob2,
    local, sent, came,
):
    far = units.bit_length() - 1
    me = lax.axis_index("seq")
    core = lax.axis_index("head")
    other = 1 - core
    x = lax.rem(me, RING)
    unit = me // RING
    tokens = RING * BLOCK
    wide = q.shape[1] // RING
    inv_scale = 1.0 / math.sqrt(HDIM)

    def columns(i, h):
        return pl.ds(pl.multiple_of(i * wide + h * HDIM, HDIM), HDIM)

    def ring_device(d):
        peer = lax.rem(x + d, RING)
        return peer, (unit * RING + peer, core)

    def send(src, dst, sem, device):
        pltpu.make_async_remote_copy(
            src_ref=src, dst_ref=dst, send_sem=sent.at[sem], recv_sem=came.at[sem],
            device_id=device, device_id_type=MESH,
        ).start()

    def scatter_cols(src, dst, h, slot):
        for d in range(1, RING):
            peer, device = ring_device(d)
            send(src.at[:, columns(peer, h)], dst.at[h, x], h * SLOTS + slot, device)
        pltpu.make_async_copy(src.at[:, columns(x, h)], dst.at[h, x], came.at[h * SLOTS + slot]).start()

    def gather_cols(src, dst, h, slot):
        for d in range(1, RING):
            peer, device = ring_device(d)
            send(src.at[h, peer], dst.at[:, columns(x, h)], h * SLOTS + slot, device)
        pltpu.make_async_copy(src.at[h, x], dst.at[:, columns(x, h)], came.at[h * SLOTS + slot]).start()

    def far_send(j, source, landing, sem):
        n = 1 << j
        group = unit // n
        base = (group + 1 - 2 * lax.rem(group, 2)) * n
        mine = lax.rem(unit, n)

        def one(i, carry):
            send(source(i), landing(mine), sem, ((base + i) * RING + x, core))
            return carry

        lax.fori_loop(0, n, one, 0)

    line = units // RING
    row = unit // line
    place = lax.rem(unit, line)
    mate = (((row + 1 - 2 * lax.rem(row, 2)) * line + place) * RING + x, core)

    def top_send(source, landing, sem):
        def one(i, carry):
            send(source(i), landing, sem, (((RING - 1 - row) * line + i) * RING + x, core))
            return carry

        lax.fori_loop(0, line, one, 0)

    def rows_at(ref, h, j, i):
        rows = BLOCK >> j
        return ref.at[h, j, pl.ds(pl.multiple_of(i * rows, rows), rows)]

    own_w = pltpu.make_async_copy(
        w.at[pl.ds(pl.multiple_of(core * (w.shape[0] // 2), 128), w.shape[0] // 2)], wv.at[0], local.at[0]
    )
    other_w = pltpu.make_async_copy(
        w.at[pl.ds(pl.multiple_of(other * (w.shape[0] // 2), 128), w.shape[0] // 2)], wv.at[1], local.at[1]
    )
    own_og = pltpu.make_async_copy(og, ogv.at[0], local.at[2])
    own_og.start()
    own_w.start()
    other_w.start()

    barrier = pltpu.get_barrier_semaphore()
    pl.semaphore_signal(barrier, inc=1, device_id=(me, other), device_id_type=MESH)
    for d in range(1, RING):
        pl.semaphore_signal(barrier, inc=1, device_id=ring_device(d)[1], device_id_type=MESH)

    def greet(d, carry):
        there = lax.rem(unit + d, units)
        pl.semaphore_signal(barrier, inc=1, device_id=(there * RING + x, core), device_id_type=MESH)
        return carry

    lax.fori_loop(1, units, greet, 0)

    first = 0
    for level in range(1, far + 2):
        count = tokens >> level
        rows = max(count, 16)
        hit = (iota((rows, tokens), 1) >> level) == iota((rows, tokens), 0)
        c01[first : first + rows, :] = jnp.where(hit, 1.0, 0.0).astype(BF16)
        first += rows
    for j in range(far):
        shape = (tokens, BLOCK)
        hit = (iota(shape, 0) >> (j + 2)) == (iota(shape, 1) & ((BLOCK >> j) - 1))
        e01[:, j * BLOCK : (j + 1) * BLOCK] = jnp.where(hit, 1.0, 0.0).astype(BF16)
    shape = (tokens, 2 * BLOCK)
    hit = (iota(shape, 0) >> 1) == iota(shape, 1)
    e01[:, far * BLOCK : (far + 2) * BLOCK] = jnp.where(hit, 1.0, 0.0).astype(BF16)

    own_og.wait()
    own_w.wait()
    dacc[...] = dot(ogv[0], wv[0])

    pl.semaphore_wait(barrier, units - 1 + RING)

    starts = [2 * BLOCK]
    for j in range(far):
        starts.append(starts[-1] + (BLOCK >> j))
    low6 = starts[far - 1] - 2 * BLOCK

    def coarse_keys(h):
        base = h * SLOTS
        arrive(kg.at[h], came.at[base + 1])
        coarse = dot(c01[2 * BLOCK :, :], kg[h].reshape(tokens, HDIM))
        for j in reversed(range(far - 1)):
            low = starts[j] - 2 * BLOCK
            ck[h, starts[j] : starts[j + 1], :] = (coarse[low : low + (BLOCK >> j)] * (1.0 / (4 << j))).astype(BF16)
            far_send(j, lambda i: ck.at[h, starts[j] : starts[j + 1]], lambda i: rows_at(kf, h, j, i), base + 5 + j)
        k6[...] = coarse[low6 : low6 + 8] * (1.0 / (4 << (far - 1)))

    def coarse_values(h):
        base = h * SLOTS
        arrive(vg.at[h], came.at[base + 2])
        coarse = dot(c01[2 * BLOCK :, :], vg[h].reshape(tokens, HDIM))
        c6[h] = jnp.concatenate([k6[...], coarse[low6 : low6 + 8]], axis=0).astype(BF16)
        top_send(lambda i: c6.at[h], f6.at[h, 0, place], base + 13)
        for j in reversed(range(far - 1)):
            low = starts[j] - 2 * BLOCK
            cv[h, starts[j] : starts[j + 1], :] = coarse[low : low + (BLOCK >> j)].astype(BF16)
            far_send(j, lambda i: cv.at[h, starts[j] : starts[j + 1]], lambda i: rows_at(vf, h, j, i), base + 9 + j)

    def top_forward(h):
        arrive(f6.at[h, 0], came.at[h * SLOTS + 13])
        send(f6.at[h, 0], f6.at[h, 1], h * SLOTS + 28, mate)

    def top_collect(h):
        arrive(g6m.at[h], came.at[h * SLOTS + 29])
        g6c[h] = (g6s[h, 0].astype(F32) + g6m[h].astype(F32)).astype(BF16)
        top_send(lambda i: g6c.at[h, i], g6r.at[h, place], h * SLOTS + 22)

    def near_rows(h):
        ck[h, : 2 * BLOCK, :] = (dot(c01[: 2 * BLOCK, :], kg[h].reshape(tokens, HDIM)) * 0.5).astype(BF16)
        cv[h, : 2 * BLOCK, :] = dot(c01[: 2 * BLOCK, :], vg[h].reshape(tokens, HDIM)).astype(BF16)

    scatter_cols(k, kg, 0, 1)
    scatter_cols(v, vg, 0, 2)
    scatter_cols(k, kg, 1, 1)
    scatter_cols(v, vg, 1, 2)
    send(ogv.at[0], ogv.at[1], 0, (me, other))
    scatter_cols(q, qg, 0, 3)
    coarse_keys(0)
    coarse_values(0)
    other_w.wait()
    arrive(ogv.at[1], came.at[0])
    dab[...] = (dacc[...] + dot(ogv[1], wv[1])).astype(BF16)
    scatter_cols(dab, ag, 0, 4)
    scatter_cols(q, qg, 1, 3)
    scatter_cols(dab, ag, 1, 4)
    near_rows(0)
    coarse_keys(1)
    top_forward(0)
    coarse_values(1)
    near_rows(1)

    pair = 2 * BLOCK
    last = (far - 1) * BLOCK

    def one_head(h):
        base = h * SLOTS
        arrive(qg.at[h], came.at[base + 3])
        arrive(ag.at[h], came.at[base + 4])
        for j in range(far - 1):
            arrive(kf.at[h, j], came.at[base + 5 + j])
            arrive(vf.at[h, j], came.at[base + 9 + j])
        arrive(f6.at[h, 1], came.at[base + 28])
        mixed = f6[h].reshape(2 * line, 16, HDIM).astype(F32)
        kf[h, far - 1] = mixed[:, :8].reshape(BLOCK, HDIM).astype(BF16)
        vf[h, far - 1] = mixed[:, 8:].reshape(BLOCK, HDIM).astype(BF16)
        far_k = kf[h].reshape(far * BLOCK, HDIM)
        far_v = vf[h].reshape(far * BLOCK, HDIM)
        sum_k = None
        sum_v = None
        for p in range(RING // 2):
            there = 1 - p
            near = slice(there * BLOCK, (there + 1) * BLOCK)
            two = slice(2 * p, 2 * p + 2)
            qp = qg[h, two].reshape(pair, HDIM)
            ap = ag[h, two].reshape(pair, HDIM)
            keys = jnp.concatenate([kg[h, two].reshape(pair, HDIM), ck[h, near, :], far_k], axis=0)
            values = jnp.concatenate([vg[h, two].reshape(pair, HDIM), cv[h, near, :], far_v], axis=0)
            scores = dot(keys, qp, ((1,), (1,))) * inv_scale
            shifted = jnp.exp(scores - jnp.max(scores, axis=0, keepdims=True))
            prob = shifted * (1.0 / jnp.sum(shifted, axis=0, keepdims=True))
            prob_low = prob.astype(BF16)
            prob_grad = dot(values, ap, ((1,), (1,)))
            centre = jnp.sum(prob * prob_grad, axis=0, keepdims=True)
            score_grad = (prob * (prob_grad - centre) * inv_scale).astype(BF16)
            attended = dot(values, prob_low, ((0,), (0,))).T
            query_grad = dot(keys, score_grad, ((0,), (0,))).T
            key_terms = dot(score_grad, qp)
            value_terms = dot(prob_low, ap)
            for s in range(2):
                rows = slice(s * BLOCK, (s + 1) * BLOCK)
                atb[h, 2 * p + s] = attended[rows].astype(BF16)
                dqb[h, 2 * p + s] = query_grad[rows].astype(BF16)
            dkl[h, p * pair : (p + 1) * pair, :] = key_terms[:pair]
            dvl[h, p * pair : (p + 1) * pair, :] = value_terms[:pair]
            g1k[h, near, :] = key_terms[pair : pair + BLOCK].astype(BF16)
            g1v[h, near, :] = value_terms[pair : pair + BLOCK].astype(BF16)
            far_terms = key_terms[pair + BLOCK :]
            sum_k = far_terms if sum_k is None else sum_k + far_terms
            far_terms = value_terms[pair + BLOCK :]
            sum_v = far_terms if sum_v is None else sum_v + far_terms
        gks[h] = sum_k[:last].astype(BF16).reshape(far - 1, BLOCK, HDIM)
        gvs[h] = sum_v[:last].astype(BF16).reshape(far - 1, BLOCK, HDIM)
        both = jnp.concatenate(
            [sum_k[last:].reshape(16, 8, HDIM), sum_v[last:].reshape(16, 8, HDIM)], axis=1
        )
        g6s[h] = both.astype(BF16).reshape(2, line, 16, HDIM)
        send(g6s.at[h, 1], g6m.at[h], base + 29, mate)
        for j in reversed(range(far - 1)):
            far_send(j, lambda i: rows_at(gks, h, j, i), lambda i: rows_at(gkr, h, j, i), base + 14 + j)
        gather_cols(atb, atg, h, 23)
        gather_cols(dqb, dq, h, 24)
        if h == 0:
            top_forward(1)
        top_collect(h)
        for j in reversed(range(far - 1)):
            far_send(j, lambda i: rows_at(gvs, h, j, i), lambda i: rows_at(gvr, h, j, i), base + 18 + j)

    def spread(h, received, near, local_sum, mean):
        pieces = []
        for j, piece in enumerate(received):
            pieces.append(piece * (1.0 / (4 << min(j, far - 1))) if mean else piece)
        piece = near[h].astype(F32)
        pieces.append(piece * 0.5 if mean else piece)
        packed = jnp.concatenate([piece.astype(BF16) for piece in pieces], axis=0)
        total = local_sum[h] + dot(e01[...], packed)
        return total.astype(BF16).reshape(RING, BLOCK, HDIM)

    def key_grads(h):
        base = h * SLOTS
        for j in range(far - 1):
            arrive(gkr.at[h, j], came.at[base + 14 + j])
        arrive(g6r.at[h], came.at[base + 22])
        mixed = g6r[h].astype(F32)[:, :8].reshape(line * 8, HDIM)
        received = [gkr[h, j].astype(F32) for j in range(far - 1)] + [mixed, jnp.zeros_like(mixed)]
        dkb[h] = spread(h, received, g1k, dkl, True)
        gather_cols(dkb, dk, h, 25)

    def value_grads(h):
        base = h * SLOTS
        for j in range(far - 1):
            arrive(gvr.at[h, j], came.at[base + 18 + j])
        mixed = g6r[h].astype(F32)[:, 8:].reshape(line * 8, HDIM)
        received = [gvr[h, j].astype(F32) for j in range(far - 1)] + [mixed, jnp.zeros_like(mixed)]
        dvb[h] = spread(h, received, g1v, dvl, False)
        gather_cols(dvb, dv, h, 26)

    one_head(0)
    one_head(1)
    key_grads(0)
    value_grads(0)

    for h in range(2):
        arrive(atb.at[h], came.at[h * SLOTS + 23])
    pob[...] = dot(atg[...], wv[1], ((1,), (1,))).astype(BF16)
    send(pob, por, 27, (me, other))
    own_out = dot(atg[...], wv[0], ((1,), (1,)))
    arrive(por, came.at[27])
    pob2[...] = (own_out + por[...].astype(F32)).astype(BF16)
    write_out = pltpu.make_async_copy(pob2, out, local.at[3])
    write_out.start()

    key_grads(1)
    value_grads(1)

    arrive(ogv.at[0], sent.at[0])
    for h in range(2):
        base = h * SLOTS
        for slot, buf in ((1, kg), (2, vg), (3, qg), (4, ag), (23, atb), (24, dqb), (25, dkb), (26, dvb)):
            arrive(buf.at[h, : RING - 1], sent.at[base + slot])
        for j in range(far - 1):
            for slot in (5, 9, 14, 18):
                arrive(kf.at[h, j], sent.at[base + slot + j])
        for slot in (13, 22, 28, 29):
            arrive(g6r.at[h], sent.at[base + slot])
        arrive(dqb.at[h], came.at[base + 24])
        arrive(dkb.at[h], came.at[base + 25])
        arrive(dvb.at[h], came.at[base + 26])
    arrive(pob, sent.at[27])
    write_out.wait()


def finish(a, b, c, d, ao, bo, co, do, buf, came, left):
    pairs = ((a, ao), (b, bo), (c, co), (d, do))
    loads = [pltpu.make_async_copy(src, buf.at[i], came.at[i]) for i, (src, _) in enumerate(pairs)]
    stores = [pltpu.make_async_copy(buf.at[i], dst, left.at[i]) for i, (_, dst) in enumerate(pairs)]
    for load in loads:
        load.start()
    for load, store in zip(loads, stores):
        load.wait()
        store.start()
    for store in stores:
        store.wait()


def on_device(queries, key_tokens, value_tokens, out_weight, output_grad):
    seq_count = lax.axis_size("seq")
    units = seq_count // RING
    far = units.bit_length() - 1
    rows, width = queries.shape
    wide = width // RING
    tokens = RING * rows
    quarter = (2, RING, BLOCK, HDIM)
    levels = (2, far - 1, BLOCK, HDIM)
    vm = pltpu.VMEM
    scratch = [
        vm((2, width, width), BF16), vm((2, rows, width), BF16), vm((rows, width), F32), vm((rows, width), BF16),
        vm(quarter, BF16), vm(quarter, BF16), vm(quarter, BF16), vm(quarter, BF16),
        vm((tokens, tokens), BF16), vm((tokens, (far + 2) * BLOCK), BF16),
        vm((2, tokens, HDIM), BF16), vm((2, tokens, HDIM), BF16), vm((8, HDIM), F32), vm((2, 16, HDIM), BF16),
        vm((2, far, BLOCK, HDIM), BF16), vm((2, far, BLOCK, HDIM), BF16), vm((2, 2, 8, 16, HDIM), BF16),
        vm(levels, BF16), vm(levels, BF16), vm((2, 2, 8, 16, HDIM), BF16),
        vm(levels, BF16), vm(levels, BF16), vm((2, 8, 16, HDIM), BF16),
        vm((2, 8, 16, HDIM), BF16), vm((2, 8, 16, HDIM), BF16),
        vm((2, 2 * BLOCK, HDIM), BF16), vm((2, 2 * BLOCK, HDIM), BF16),
        vm((2, tokens, HDIM), F32), vm((2, tokens, HDIM), F32),
        vm(quarter, BF16), vm(quarter, BF16), vm(quarter, BF16), vm(quarter, BF16),
        vm((rows, width), BF16), vm((rows, width), BF16), vm((rows, width), BF16), vm((rows, width), BF16),
        pltpu.SemaphoreType.DMA((4,)), pltpu.SemaphoreType.DMA((2 * SLOTS,)), pltpu.SemaphoreType.DMA((2 * SLOTS,)),
    ]
    anywhere = pl.BlockSpec(memory_space=pl.ANY)
    shapes = [jax.ShapeDtypeStruct((rows, width), BF16)] * 4
    results = pl.pallas_call(
        functools.partial(kernel, units),
        out_shape=shapes,
        in_specs=[anywhere] * 5,
        out_specs=[anywhere] * 4,
        scratch_shapes=scratch,
        compiler_params=pltpu.CompilerParams(
            collective_id=0, has_side_effects=True, vmem_limit_bytes=60 * 1024 * 1024
        ),
        name="layer",
    )(queries, key_tokens, value_tokens, out_weight, output_grad)
    return pl.pallas_call(
        finish,
        out_shape=shapes,
        in_specs=[anywhere] * 4,
        out_specs=[anywhere] * 4,
        scratch_shapes=[
            vm((4, rows, width), BF16), pltpu.SemaphoreType.DMA((4,)), pltpu.SemaphoreType.DMA((4,)),
        ],
        name="finish",
    )(*results)


def solution(mesh):
    placed = (P("seq", "head"), P("seq", "head"), P("seq", "head"), P(None, "head"), P("seq", "head"))
    return jax.shard_map(
        on_device,
        mesh=mesh,
        in_specs=placed,
        out_specs=(P("seq", "head"),) * 4,
        check_vma=False,
    )
```
